32 devices in a mesh: region: 16 (over z, y, x), mp: 2 (over core).
Axes of the slice: x: 2, y: 2, z: 4, core: 2. Of those that a mesh axis runs over, the one named last changes fastest.
Arguments:
- tokens: bfloat16 [16384, 1024], P('region')
- ln_gain: bfloat16 [1024], replicated, may hold values from 0.25 to 1.75
- w_qkv: bfloat16 [1024, 3, 1024], P(None, None, 'mp')
- w_out: bfloat16 [1024, 1024], P('mp'), may hold values from -0.75 to 0.75
- neighbours: int32 [256, 8], P('region'), may hold values from 0 to 255, as said below
- degree: int32 [256], P('region'), may hold values from 1 to 8
Outputs:
- update: bfloat16 [16384, 1024], P('region')
The draws below stay inside these ranges and needn't reach their ends.
Inputs may be any that keep to these rules, and one draw needn't show every extreme that they name: A neighbour of a patch with local index below 2 in its region (local index = id % 16, region = id // 16) lies in the same region or is one of the last 2 patches of region r-1 or r-2 (cyclically); of local index 14 or more: same region or one of the first 2 patches of region r+1 or r+2; any other patch's neighbours lie in its own region. Only the first degree[p] entries of a row count.
All inputs are finite; a program needn't handle non-finite values.
Results may differ from the reference program's by a relative error of at most 0.012.
The reference program's roundings to bfloat16 on the way (of `normed`, `weights` and `context`) count: a program that leaves them out, or rounds other values in their place, can miss the bound.
Values may be sent and summed in bfloat16 or wider, within the bound.
A program may use at most 192 MiB of HBM per device.

```python
import jax
import jax.numpy as jnp
from jax import lax

D = 1024
HEADS = 16
HDIM = 64
PATCH = 64
NBR = 8
RIM = 2
PD = 16
PATCHES = 256
TOKENS = 16384
N_REGION = 16


def draw_tokens(key, part):
    base = jax.random.normal(key, (TOKENS, D), jnp.float32)
    return base.astype(jnp.bfloat16)


def draw_w_qkv(key, part):
    base = jax.random.normal(key, (D, 3, D), jnp.float32) * D ** (-0.5)
    return base.astype(jnp.bfloat16)


def draw_neighbours(key, part):
    patch_ids = jnp.arange(PATCHES, dtype=jnp.int32)[:, None]
    region_of = patch_ids // PD
    local_of = patch_ids % PD
    selector = jax.random.randint(jax.random.fold_in(key, 31), (PATCHES, NBR), 0, 3)
    own_pick = jax.random.randint(jax.random.fold_in(key, 32), (PATCHES, NBR), 0, PD)
    rim_pick = jax.random.randint(jax.random.fold_in(key, 33), (PATCHES, NBR), 0, RIM)
    lower = local_of < RIM
    upper = local_of >= PD - RIM
    reach = jnp.where(lower, -selector, jnp.where(upper, selector, 0))
    owner = (region_of + reach) % N_REGION
    local = jnp.where(reach < 0, PD - RIM + rim_pick, jnp.where(reach > 0, rim_pick, own_pick))
    return (owner * PD + local).astype(jnp.int32)


def touch_ends(entries, own_key, least, high):
    place = [jax.random.randint(jax.random.fold_in(own_key, axis), (), 0, length) for axis, length in enumerate(entries.shape)]
    main_axis = entries.shape.index(max(entries.shape))
    beside = place[:main_axis] + [(place[main_axis] + 1) % entries.shape[main_axis]] + place[main_axis + 1:]
    return entries.at[tuple(place)].set(least).at[tuple(beside)].set(high)


def levels(stream_key, shape, shards, smallest, top_value):
    factor_of, own = 1.0, jax.random.fold_in(stream_key, 6)
    for dim, blocks in shards:
        draws = jnp.exp(jax.random.uniform(jax.random.fold_in(own, dim), (blocks,), jnp.float32, smallest / len(shards), top_value / len(shards)))
        factor_of = factor_of * jnp.repeat(draws, shape[dim] // blocks).reshape([-1 if axis == dim else 1 for axis in range(len(shape))])
    return factor_of


def normal_values(stream_key, extent, width, bound, cuts=(), held_as=jnp.bfloat16):
    entries = width * jax.random.normal(stream_key, extent, jnp.float32)
    if cuts:
        entries = entries * levels(stream_key, extent, cuts, -0.22, 0.18)
    return jnp.clip(entries, -bound, bound).astype(held_as)


def setup_inputs(seed: int = 0) -> dict:
    seeds = jax.random.split(jax.random.key(seed), 7)
    return {
        "tokens": draw_tokens(jax.random.fold_in(seeds[6], 71), 0),
        "ln_gain": jnp.clip(1.0 + 0.15 * jax.random.normal(seeds[1], (D,), jnp.float32), 0.25, 1.75).astype(jnp.bfloat16),
        "w_qkv": draw_w_qkv(jax.random.fold_in(seeds[6], 71), 0),
        "w_out": normal_values(seeds[3], (D, D), (D // 16) ** -0.5, 0.75, ((0, 2),)),
        "neighbours": draw_neighbours(jax.random.fold_in(seeds[6], 71), 0),
        "degree": touch_ends(jax.random.randint(seeds[5], (PATCHES,), 1, NBR + 1), jax.random.fold_in(seeds[5], 1), 1, NBR).astype(jnp.int32),
    }


def layer_norm(rows, gain):
    values = rows.astype(jnp.float32)
    centre = lax.optimization_barrier(jnp.mean(values, axis=-1, keepdims=True))
    spread = lax.optimization_barrier(jnp.mean((values - centre) ** 2, axis=-1, keepdims=True))
    return ((values - centre) * lax.rsqrt(spread + 1e-05) * gain.astype(jnp.float32)).astype(jnp.bfloat16)

def attend_block(query, pairs, valid, heads):
    npat, keys = (pairs.shape[0], pairs.shape[1])
    patch = query.shape[1]
    query = query.reshape(npat, patch, heads, HDIM).astype(jnp.float32)
    key_part = pairs[:, :, 0, :].reshape(npat, keys, heads, HDIM).astype(jnp.float32)
    value_part = pairs[:, :, 1, :].reshape(npat, keys, heads, HDIM).astype(jnp.float32)
    scores = jnp.einsum('pqhd,pkhd->phqk', query, key_part)
    scores = jnp.where(valid[:, None, None, :], scores, jnp.float32(-1e+30))
    top = lax.optimization_barrier(jnp.max(scores, axis=-1, keepdims=True))
    expo = jnp.exp(scores - top)
    total = lax.optimization_barrier(jnp.sum(expo, axis=-1))
    weights = expo.astype(jnp.bfloat16).astype(jnp.float32)
    context = jnp.einsum('phqk,pkhd->pqhd', weights, value_part)
    context = context / jnp.transpose(total, (0, 2, 1))[..., None]
    return context.astype(jnp.bfloat16).reshape(npat * patch, heads * HDIM)

def reference(tokens, ln_gain, w_qkv, w_out, neighbours, degree):
    normed = layer_norm(tokens, ln_gain)
    w_flat = w_qkv.reshape(D, 3 * D)
    scale = 1.0 / HDIM ** 0.5

    def project(block):
        out = jnp.dot(block, w_flat, preferred_element_type=jnp.float32).reshape(-1, 3, D)
        query = (out[:, 0, :] * scale).astype(jnp.bfloat16)
        pair = jnp.stack([out[:, 1, :].astype(jnp.bfloat16), out[:, 2, :].astype(jnp.bfloat16)], axis=1)
        return (query, pair)
    q_all, kv_all = lax.map(project, normed.reshape(N_REGION, PD * PATCH, D))
    kv_pat = kv_all.reshape(PATCHES, PATCH, 2, D)
    anchor = kv_pat[0]

    def block_update(items):
        query, nbr, deg, region_id = items
        own = lax.dynamic_slice_in_dim(kv_pat, (region_id * PD).astype(jnp.int32), PD, 0)
        far = kv_pat[nbr].reshape(PD, NBR * PATCH, 2, D)
        anchors = jnp.broadcast_to(anchor[None], (PD, PATCH, 2, D))
        pairs = jnp.concatenate([own, far, anchors], axis=1)
        slot_ok = jnp.arange(NBR, dtype=jnp.int32)[None, :] < deg[:, None]
        far_ok = jnp.repeat(slot_ok, PATCH, axis=1)
        ones = jnp.ones((PD, PATCH), dtype=bool)
        valid = jnp.concatenate([ones, far_ok, ones], axis=1)
        context = attend_block(query.reshape(PD, PATCH, D), pairs, valid, HEADS)
        return jnp.dot(context, w_out, preferred_element_type=jnp.float32).astype(jnp.bfloat16)
    region_ids = jnp.arange(N_REGION, dtype=jnp.int32)
    result = lax.map(block_update, (q_all, neighbours.reshape(N_REGION, PD, NBR), degree.reshape(N_REGION, PD), region_ids))
    return result.reshape(TOKENS, D)
```

```python
import functools
import math

import jax
import jax.numpy as jnp
from jax import lax
from jax.experimental import pallas as pl
from jax.experimental.pallas import tpu as pltpu
from jax.sharding import PartitionSpec as P

HDIM = 64
NBR = 8
RIM = 2
GROUP = 4
MESH = pl.DeviceIdType.MESH


def kernel(
    n,
    tok_hbm,
    gain_ref,
    wqkv_hbm,
    wout_hbm,
    nbr_ref,
    deg_ref,
    out_hbm,
    tok,
    wqkv,
    wout,
    far_raw,
    anc_raw,
    q_tab,
    k_tab,
    v_tab,
    ctx,
    out,
    load_sem,
    anc_sem,
    anc_send,
    anc_recv,
    pair_send,
    pair_recv,
    far_send,
    far_recv,
    fwd_send,
    fwd_recv,
    ctx_send,
    ctx_recv,
    out_sem,
):
    rows, width = tok.shape
    patch = far_raw.shape[1]
    npat = rows // patch
    feat = q_tab.shape[1]
    half = patch // 2
    levels = max(1, math.ceil(math.log2(n)))
    far_n = 4 * RIM
    anchor_slot = npat + far_n
    region = lax.axis_index("region")
    core = lax.axis_index("mp")
    other = 1 - core

    chunk = 2 * patch
    nchunk = rows // chunk
    loads = [pltpu.make_async_copy(tok_hbm, tok, load_sem.at[0])]
    for j in range(3):
        loads.append(pltpu.make_async_copy(wqkv_hbm.at[j], wqkv.at[j], load_sem.at[1 + j]))
    loads.append(pltpu.make_async_copy(wout_hbm, wout.at[core], load_sem.at[4]))
    for c in loads:
        c.start()

    ring = [lax.rem(region + d + n, n) for d in (1, 2, -1, -2)]
    has_child, has_parent = [], []
    for j in range(levels):
        step, span = 2**j, 2 ** (j + 1)
        has_child.append(jnp.logical_and(lax.rem(region, span) == 0, region + step < n))
        has_parent.append(lax.rem(region, span) == step)

    depth = jnp.int32(0)
    for j in range(levels):
        depth = depth + lax.rem(region // (2**j), 2)

    barrier = pltpu.get_barrier_semaphore()
    for target in ring:
        pl.semaphore_signal(barrier, inc=1, device_id=(target, core), device_id_type=MESH)
    pl.semaphore_signal(barrier, inc=1, device_id=(region, other), device_id_type=MESH)
    links = jnp.int32(5)
    for j in range(levels):
        links = links + has_child[j].astype(jnp.int32) + has_parent[j].astype(jnp.int32)

        @pl.when(has_child[j])
        def _():
            pl.semaphore_signal(barrier, inc=1, device_id=(region + 2**j, core), device_id_type=MESH)

        @pl.when(has_parent[j])
        def _():
            pl.semaphore_signal(barrier, inc=1, device_id=(region - 2**j, core), device_id_type=MESH)

    pl.semaphore_wait(barrier, links)

    def anc_copy(j):
        return pltpu.make_async_remote_copy(
            src_ref=anc_raw.at[core],
            dst_ref=anc_raw.at[core],
            send_sem=anc_send.at[j],
            recv_sem=anc_recv,
            device_id=(lax.rem(region + 2**j, n), core),
            device_id_type=MESH,
        )

    def pair_copy(which):
        return pltpu.make_async_remote_copy(
            src_ref=anc_raw.at[which],
            dst_ref=anc_raw.at[which],
            send_sem=pair_send.at[0],
            recv_sem=pair_recv.at[0],
            device_id=(region, other),
            device_id_type=MESH,
        )

    def wout_copy(which):
        return pltpu.make_async_remote_copy(
            src_ref=wout_hbm,
            dst_ref=wout.at[which],
            send_sem=pair_send.at[1],
            recv_sem=pair_recv.at[1],
            device_id=(region, other),
            device_id_type=MESH,
        )

    def far_copy(d):
        first = (npat - RIM if d < 2 else 0) + core
        return pltpu.make_async_remote_copy(
            src_ref=tok_hbm.at[pl.ds(pl.multiple_of(first * patch, patch), patch)],
            dst_ref=far_raw.at[d * RIM + core],
            send_sem=far_send.at[d],
            recv_sem=far_recv.at[d],
            device_id=(ring[d], core),
            device_id_type=MESH,
        )

    def fwd_copy(d, which):
        return pltpu.make_async_remote_copy(
            src_ref=far_raw.at[d * RIM + which],
            dst_ref=far_raw.at[d * RIM + which],
            send_sem=fwd_send.at[d],
            recv_sem=fwd_recv.at[d],
            device_id=(region, other),
            device_id_type=MESH,
        )

    size = GROUP * patch

    def ctx_copy(g, which):
        span = pl.ds(pl.multiple_of(g * size, size), size)
        return pltpu.make_async_remote_copy(
            src_ref=ctx.at[which, span],
            dst_ref=ctx.at[which, span],
            send_sem=ctx_send.at[g],
            recv_sem=ctx_recv.at[g],
            device_id=(region, other),
            device_id_type=MESH,
        )

    def pass_anchor():
        @pl.when(region == 0)
        def _():
            mine = pltpu.make_async_copy(
                tok_hbm.at[pl.ds(pl.multiple_of(core * half, half), half)], anc_raw.at[core], anc_sem
            )
            mine.start()
            mine.wait()

        @pl.when(region > 0)
        def _():
            anc_copy(0).wait_recv()

        for j in reversed(range(levels)):

            @pl.when(has_child[j])
            def _():
                anc_copy(j).start()

        pair_copy(core).start()
        for d in range(4):
            far_copy(d).start()

    wout_copy(core).start()

    gain = gain_ref[...].astype(jnp.float32)

    def normalise(raw):
        values = raw.astype(jnp.float32)
        centre = jnp.mean(values, axis=-1, keepdims=True)
        away = values - centre
        spread = jnp.mean(away * away, axis=-1, keepdims=True)
        return (away * lax.rsqrt(spread + 1e-05) * gain).astype(jnp.bfloat16)

    def key_value(normed, first, count):
        for tab, j in ((k_tab, 1), (v_tab, 2)):
            part = jnp.dot(normed, wqkv[j], preferred_element_type=jnp.float32)
            tab[pl.ds(first, count)] = part.astype(jnp.bfloat16).reshape(count, patch, feat)

    for c in loads:
        c.wait()

    def qkv_step(i, carry):
        span = pl.ds(pl.multiple_of(i * chunk, chunk), chunk)
        normed = normalise(tok[span])
        part = jnp.dot(normed, wqkv[0], preferred_element_type=jnp.float32)
        q_tab[span] = (part * (1.0 / HDIM**0.5)).astype(jnp.bfloat16)
        key_value(normed, i * 2, 2)

        @pl.when(i == jnp.minimum(depth * 2, nchunk - 1))
        def _():
            pass_anchor()

        return carry

    lax.fori_loop(0, nchunk, qkv_step, 0)

    pair_copy(other).wait_recv()
    key_value(normalise(anc_raw[...].reshape(patch, width)), anchor_slot, 1)

    block = GROUP * HDIM
    keys = (NBR + 2) * patch
    lane = lax.broadcasted_iota(jnp.int32, (patch, block), 1) // HDIM
    column = lax.broadcasted_iota(jnp.int32, (1, keys), 1)

    def attend(t):
        p = lax.rem(t + RIM, npat)
        deg = deg_ref[p]
        slots = [p]
        for j in range(NBR):
            nb = nbr_ref[j, p]
            owner, local = nb // npat, lax.rem(nb, npat)
            reach = lax.rem(owner - region + n, n)
            slot = jnp.where(
                reach == 0,
                local,
                jnp.where(
                    reach == n - 1,
                    local + RIM,
                    jnp.where(
                        reach == n - 2,
                        local + 2 * RIM,
                        jnp.where(reach == 1, npat + 2 * RIM + local, npat + 3 * RIM + local),
                    ),
                ),
            )
            slots.append(jnp.where(j < deg, slot, p))
        slots.append(anchor_slot)
        valid = jnp.logical_or(column < (deg + 1) * patch, column >= (NBR + 1) * patch)
        at = pl.ds(pl.multiple_of(p * patch, patch), patch)
        to = pl.ds(pl.multiple_of(t * patch, patch), patch)
        for b in range(feat // block):
            cols = slice(b * block, (b + 1) * block)
            qb = q_tab[at, cols]
            zero = jnp.zeros_like(qb)
            spread = jnp.concatenate([jnp.where(lane == i, qb, zero) for i in range(GROUP)], axis=0)
            kk = jnp.concatenate([k_tab[s, :, cols] for s in slots], axis=0)
            vv = jnp.concatenate([v_tab[s, :, cols] for s in slots], axis=0)
            scores = lax.dot_general(
                spread, kk, (((1,), (1,)), ((), ())), preferred_element_type=jnp.float32
            )
            scores = jnp.where(valid, scores, jnp.float32(-1e30))
            top = jnp.max(scores, axis=-1, keepdims=True)
            expo = jnp.exp(scores - top)
            total = jnp.sum(expo, axis=-1, keepdims=True)
            mixed = jnp.dot(expo.astype(jnp.bfloat16), vv, preferred_element_type=jnp.float32) / total
            packed = jnp.where(lane == 0, mixed[:patch], 0.0)
            for i in range(1, GROUP):
                packed = jnp.where(lane == i, mixed[i * patch : (i + 1) * patch], packed)
            ctx[core, to, cols] = packed.astype(jnp.bfloat16)

    rim_rows = RIM * patch

    def project(g):
        span = pl.ds(pl.multiple_of(g * size, size), size)
        ctx_copy(g, other).wait_recv()
        total = jnp.dot(ctx[0, span], wout[0], preferred_element_type=jnp.float32)
        total = total + jnp.dot(ctx[1, span], wout[1], preferred_element_type=jnp.float32)
        out[span] = total.astype(jnp.bfloat16)

    def inner_out(g):
        return pltpu.make_async_copy(
            out.at[pl.ds(pl.multiple_of(g * size, size), size)],
            out_hbm.at[pl.ds(pl.multiple_of(g * size + rim_rows, rim_rows), size)],
            out_sem.at[g],
        )

    ngroup = npat // GROUP

    def group_step(g, carry):
        @pl.when(g == 1)
        def _():
            for d in range(4):
                far_copy(d).wait_recv()
                fwd_copy(d, core).start()
            wout_copy(other).wait_recv()

        @pl.when(g == ngroup - 1)
        def _():
            for d in range(4):
                fwd_copy(d, other).wait_recv()

            def far_step(d, c):
                raw = far_raw[pl.ds(d * RIM, RIM)].reshape(rim_rows, width)
                key_value(normalise(raw), npat + d * RIM, RIM)
                return c

            lax.fori_loop(0, 4, far_step, 0)

        def patch_step(u, c):
            attend(g * GROUP + u)
            return c

        lax.fori_loop(0, GROUP, patch_step, 0)
        ctx_copy(g, core).start()

        @pl.when(g >= 1)
        def _():
            project(g - 1)
            inner_out(g - 1).start()

        return carry

    lax.fori_loop(0, ngroup, group_step, 0)
    project(ngroup - 1)
    tail = rows - size
    last = [
        pltpu.make_async_copy(
            out.at[pl.ds(tail, rim_rows)], out_hbm.at[pl.ds(rows - rim_rows, rim_rows)], out_sem.at[ngroup - 1]
        ),
        pltpu.make_async_copy(
            out.at[pl.ds(tail + rim_rows, rim_rows)], out_hbm.at[pl.ds(0, rim_rows)], out_sem.at[ngroup]
        ),
    ]
    for c in last:
        c.start()

    for j in range(levels):

        @pl.when(has_child[j])
        def _():
            anc_copy(j).wait_send()

    pair_copy(core).wait_send()
    wout_copy(core).wait_send()
    for d in range(4):
        far_copy(d).wait_send()
        fwd_copy(d, core).wait_send()
    for g in range(ngroup):
        ctx_copy(g, core).wait_send()
    for g in range(ngroup - 1):
        inner_out(g).wait()
    for c in last:
        c.wait()


def solution(mesh):
    n = mesh.shape["region"]

    def per_device(tokens, ln_gain, w_qkv, w_out, neighbours, degree):
        rows, width = tokens.shape
        npat = neighbours.shape[0]
        patch = rows // npat
        feat = w_qkv.shape[2]
        levels = max(1, math.ceil(math.log2(n)))
        ngroup = npat // GROUP
        slots = npat + 4 * RIM + 1
        any_spec = pl.BlockSpec(memory_space=pl.ANY)
        smem = pl.BlockSpec(memory_space=pltpu.SMEM)
        dma = pltpu.SemaphoreType.DMA
        bf = jnp.bfloat16
        return pl.pallas_call(
            functools.partial(kernel, n),
            out_shape=jax.ShapeDtypeStruct((rows, width), bf),
            in_specs=[
                any_spec,
                pl.BlockSpec(memory_space=pltpu.VMEM),
                any_spec,
                any_spec,
                smem,
                smem,
            ],
            out_specs=any_spec,
            scratch_shapes=[
                pltpu.VMEM((rows, width), bf),
                pltpu.VMEM((3, width, feat), bf),
                pltpu.VMEM((2, feat, width), bf),
                pltpu.VMEM((4 * RIM, patch, width), bf),
                pltpu.VMEM((2, patch // 2, width), bf),
                pltpu.VMEM((rows, feat), bf),
                pltpu.VMEM((slots, patch, feat), bf),
                pltpu.VMEM((slots, patch, feat), bf),
                pltpu.VMEM((2, rows, feat), bf),
                pltpu.VMEM((rows, width), bf),
                dma((5,)),
                dma,
                dma((levels,)),
                dma,
                dma((2,)),
                dma((2,)),
                dma((4,)),
                dma((4,)),
                dma((4,)),
                dma((4,)),
                dma((ngroup,)),
                dma((ngroup,)),
                dma((ngroup + 1,)),
            ],
            compiler_params=pltpu.CompilerParams(
                collective_id=0, has_side_effects=True, vmem_limit_bytes=56 * 2**20
            ),
            name="patch_attention",
        )(
            tokens,
            ln_gain.reshape(1, width),
            jnp.transpose(w_qkv, (1, 0, 2)),
            w_out,
            jnp.transpose(neighbours),
            degree,
        )

    placed = (
        P("region", None),
        P(),
        P(None, None, "mp"),
        P("mp", None),
        P("region", None),
        P("region"),
    )
    return jax.shard_map(
        per_device, mesh=mesh, in_specs=placed, out_specs=P("region", None), check_vma=False
    )
```

```python
import functools

import jax
import jax.numpy as jnp
from jax import lax
from jax.experimental import pallas as pl
from jax.experimental.pallas import tpu as pltpu
from jax.sharding import PartitionSpec as P

HDIM = 64
NBR = 8
RIM = 2
GROUP = 4
FAN = 4
EARLY = 2
MESH = pl.DeviceIdType.MESH


def tree_levels(n):
    levels = 1
    while FAN**levels < n:
        levels += 1
    return levels


def kernel(
    n,
    tok_hbm,
    gain_ref,
    wqkv_hbm,
    wout_hbm,
    nbr_ref,
    deg_ref,
    out_hbm,
    tok,
    wqkv,
    wout,
    far_raw,
    anc_raw,
    q_tab,
    k_tab,
    v_tab,
    ctx,
    out,
    load_sem,
    anc_sem,
    anc_send,
    anc_recv,
    pair_send,
    pair_recv,
    far_send,
    far_recv,
    fwd_send,
    fwd_recv,
    ctx_send,
    ctx_recv,
    out_sem,
):
    rows, width = tok.shape
    patch = far_raw.shape[1]
    npat = rows // patch
    feat = q_tab.shape[1]
    half = patch // 2
    levels = tree_levels(n)
    far_n = 4 * RIM
    anchor_slot = npat + far_n
    region = lax.axis_index("region")
    core = lax.axis_index("mp")
    other = 1 - core

    chunk = 2 * patch
    nchunk = rows // chunk
    loads = [pltpu.make_async_copy(tok_hbm, tok, load_sem.at[0])]
    for j in range(3):
        loads.append(pltpu.make_async_copy(wqkv_hbm.at[j], wqkv.at[j], load_sem.at[1 + j]))
    loads.append(pltpu.make_async_copy(wout_hbm, wout.at[core], load_sem.at[4]))
    for c in loads:
        c.start()

    ring = [lax.rem(region + d + n, n) for d in (1, 2, -1, -2)]
    children, parents = [], []
    depth = jnp.int32(0)
    for level in range(levels):
        step = FAN**level
        digit = lax.rem(region // step, FAN)
        depth = depth + (digit > 0).astype(jnp.int32)
        alone = lax.rem(region, step) == 0
        for j in range(1, FAN):
            target = region + j * step
            children.append((jnp.logical_and(lax.rem(region, step * FAN) == 0, target < n), target))
            parents.append((jnp.logical_and(alone, digit == j), region - j * step))
    near = region < EARLY

    barrier = pltpu.get_barrier_semaphore()
    for target in ring:
        pl.semaphore_signal(barrier, inc=1, device_id=(target, core), device_id_type=MESH)
    pl.semaphore_signal(barrier, inc=1, device_id=(region, other), device_id_type=MESH)
    links = jnp.int32(5)
    for there, target in children + parents:
        links = links + there.astype(jnp.int32)

        @pl.when(there)
        def _():
            pl.semaphore_signal(barrier, inc=1, device_id=(target, core), device_id_type=MESH)

    def anc_copy(j):
        return pltpu.make_async_remote_copy(
            src_ref=anc_raw.at[core],
            dst_ref=anc_raw.at[core],
            send_sem=anc_send.at[j],
            recv_sem=anc_recv,
            device_id=(lax.rem(children[j][1], n), core),
            device_id_type=MESH,
        )

    def pair_copy(which):
        return pltpu.make_async_remote_copy(
            src_ref=anc_raw.at[which],
            dst_ref=anc_raw.at[which],
            send_sem=pair_send.at[0],
            recv_sem=pair_recv.at[0],
            device_id=(region, other),
            device_id_type=MESH,
        )

    def wout_copy(which):
        return pltpu.make_async_remote_copy(
            src_ref=wout_hbm,
            dst_ref=wout.at[which],
            send_sem=pair_send.at[1],
            recv_sem=pair_recv.at[1],
            device_id=(region, other),
            device_id_type=MESH,
        )

    def far_copy(d):
        first = (npat - RIM if d < 2 else 0) + core
        return pltpu.make_async_remote_copy(
            src_ref=tok_hbm.at[pl.ds(pl.multiple_of(first * patch, patch), patch)],
            dst_ref=far_raw.at[d * RIM + core],
            send_sem=far_send.at[d],
            recv_sem=far_recv.at[d],
            device_id=(ring[d], core),
            device_id_type=MESH,
        )

    def fwd_copy(d, which):
        return pltpu.make_async_remote_copy(
            src_ref=far_raw.at[d * RIM + which],
            dst_ref=far_raw.at[d * RIM + which],
            send_sem=fwd_send.at[d],
            recv_sem=fwd_recv.at[d],
            device_id=(region, other),
            device_id_type=MESH,
        )

    size = GROUP * patch

    def ctx_copy(g, which):
        span = pl.ds(pl.multiple_of(g * size, size), size)
        return pltpu.make_async_remote_copy(
            src_ref=ctx.at[which, span],
            dst_ref=ctx.at[which, span],
            send_sem=ctx_send.at[g],
            recv_sem=ctx_recv.at[g],
            device_id=(region, other),
            device_id_type=MESH,
        )

    def send_anchor():
        for j in reversed(range(len(children))):

            @pl.when(children[j][0])
            def _():
                anc_copy(j).start()

        pair_copy(core).start()

    def send_far():
        for d in range(4):
            far_copy(d).start()

    def enter():
        pl.semaphore_wait(barrier, links)

        @pl.when(region == 0)
        def _():
            mine = pltpu.make_async_copy(
                tok_hbm.at[pl.ds(pl.multiple_of(core * half, half), half)], anc_raw.at[core], anc_sem
            )
            mine.start()
            mine.wait()
            send_anchor()

        send_far()
        wout_copy(core).start()

    def relay():
        anc_copy(0).wait_recv()
        send_anchor()

    gain = gain_ref[...].astype(jnp.float32)

    def normalise(raw):
        values = raw.astype(jnp.float32)
        centre = jnp.mean(values, axis=-1, keepdims=True)
        away = values - centre
        spread = jnp.mean(away * away, axis=-1, keepdims=True)
        return (away * lax.rsqrt(spread + 1e-05) * gain).astype(jnp.bfloat16)

    def key_value(normed, first, count):
        for tab, j in ((k_tab, 1), (v_tab, 2)):
            part = jnp.dot(normed, wqkv[j], preferred_element_type=jnp.float32)
            tab[pl.ds(first, count)] = part.astype(jnp.bfloat16).reshape(count, patch, feat)

    enter_at = jnp.where(near, nchunk - 1, 0)
    relay_at = jnp.where(near, nchunk - 1, jnp.minimum(3 * depth, nchunk - 1))

    def qkv_step(i, carry):
        @pl.when(i == enter_at)
        def _():
            enter()

        @pl.when(i == 0)
        def _():
            for c in loads:
                c.wait()

        span = pl.ds(pl.multiple_of(i * chunk, chunk), chunk)
        normed = normalise(tok[span])
        part = jnp.dot(normed, wqkv[0], preferred_element_type=jnp.float32)
        q_tab[span] = (part * (1.0 / HDIM**0.5)).astype(jnp.bfloat16)
        key_value(normed, i * 2, 2)

        @pl.when(jnp.logical_and(i == relay_at, region > 0))
        def _():
            relay()

        return carry

    lax.fori_loop(0, nchunk, qkv_step, 0)

    pair_copy(other).wait_recv()
    key_value(normalise(anc_raw[...].reshape(patch, width)), anchor_slot, 1)

    block = GROUP * HDIM
    keys = (NBR + 2) * patch
    lane = lax.broadcasted_iota(jnp.int32, (patch, block), 1) // HDIM
    column = lax.broadcasted_iota(jnp.int32, (1, keys), 1)

    def attend(t):
        p = lax.rem(t + RIM, npat)
        deg = deg_ref[p]
        slots = [p]
        for j in range(NBR):
            nb = nbr_ref[j, p]
            owner, local = nb // npat, lax.rem(nb, npat)
            reach = lax.rem(owner - region + n, n)
            slot = jnp.where(
                reach == 0,
                local,
                jnp.where(
                    reach == n - 1,
                    local + RIM,
                    jnp.where(
                        reach == n - 2,
                        local + 2 * RIM,
                        jnp.where(reach == 1, npat + 2 * RIM + local, npat + 3 * RIM + local),
                    ),
                ),
            )
            slots.append(jnp.where(j < deg, slot, p))
        slots.append(anchor_slot)
        valid = jnp.logical_or(column < (deg + 1) * patch, column >= (NBR + 1) * patch)
        at = pl.ds(pl.multiple_of(p * patch, patch), patch)
        to = pl.ds(pl.multiple_of(t * patch, patch), patch)
        for b in range(feat // block):
            cols = slice(b * block, (b + 1) * block)
            qb = q_tab[at, cols]
            zero = jnp.zeros_like(qb)
            spread = jnp.concatenate([jnp.where(lane == i, qb, zero) for i in range(GROUP)], axis=0)
            kk = jnp.concatenate([k_tab[s, :, cols] for s in slots], axis=0)
            vv = jnp.concatenate([v_tab[s, :, cols] for s in slots], axis=0)
            scores = lax.dot_general(
                spread, kk, (((1,), (1,)), ((), ())), preferred_element_type=jnp.float32
            )
            scores = jnp.where(valid, scores, jnp.float32(-1e30))
            top = jnp.max(scores, axis=-1, keepdims=True)
            expo = jnp.exp(scores - top)
            total = jnp.sum(expo, axis=-1, keepdims=True)
            mixed = jnp.dot(expo.astype(jnp.bfloat16), vv, preferred_element_type=jnp.float32) / total
            packed = jnp.where(lane == 0, mixed[:patch], 0.0)
            for i in range(1, GROUP):
                packed = jnp.where(lane == i, mixed[i * patch : (i + 1) * patch], packed)
            ctx[core, to, cols] = packed.astype(jnp.bfloat16)

    rim_rows = RIM * patch

    def project(g):
        span = pl.ds(pl.multiple_of(g * size, size), size)
        ctx_copy(g, other).wait_recv()
        total = jnp.dot(ctx[0, span], wout[0], preferred_element_type=jnp.float32)
        total = total + jnp.dot(ctx[1, span], wout[1], preferred_element_type=jnp.float32)
        out[span] = total.astype(jnp.bfloat16)

    def inner_out(g):
        return pltpu.make_async_copy(
            out.at[pl.ds(pl.multiple_of(g * size, size), size)],
            out_hbm.at[pl.ds(pl.multiple_of(g * size + rim_rows, rim_rows), size)],
            out_sem.at[g],
        )

    ngroup = npat // GROUP

    def swap_far():
        for d in range(4):
            far_copy(d).wait_recv()
            fwd_copy(d, core).start()
        wout_copy(other).wait_recv()

    def far_step(d, c):
        raw = far_raw[pl.ds(d * RIM, RIM)].reshape(rim_rows, width)
        key_value(normalise(raw), npat + d * RIM, RIM)
        return c

    def group_step(g, carry):
        @pl.when(g == 1)
        def _():
            swap_far()

        @pl.when(g == ngroup - 1)
        def _():
            for d in range(4):
                fwd_copy(d, other).wait_recv()
            lax.fori_loop(0, 4, far_step, 0)

        def patch_step(u, c):
            attend(g * GROUP + u)
            return c

        lax.fori_loop(0, GROUP, patch_step, 0)
        ctx_copy(g, core).start()

        @pl.when(g >= 1)
        def _():
            project(g - 1)
            inner_out(g - 1).start()

        return carry

    lax.fori_loop(0, ngroup, group_step, 0)
    project(ngroup - 1)
    tail = rows - size
    last = [
        pltpu.make_async_copy(
            out.at[pl.ds(tail, rim_rows)], out_hbm.at[pl.ds(rows - rim_rows, rim_rows)], out_sem.at[ngroup - 1]
        ),
        pltpu.make_async_copy(
            out.at[pl.ds(tail + rim_rows, rim_rows)], out_hbm.at[pl.ds(0, rim_rows)], out_sem.at[ngroup]
        ),
    ]
    for c in last:
        c.start()

    for j in range(len(children)):

        @pl.when(children[j][0])
        def _():
            anc_copy(j).wait_send()

    pair_copy(core).wait_send()
    wout_copy(core).wait_send()
    for d in range(4):
        far_copy(d).wait_send()
        fwd_copy(d, core).wait_send()
    for g in range(ngroup):
        ctx_copy(g, core).wait_send()
    for g in range(ngroup - 1):
        inner_out(g).wait()
    for c in last:
        c.wait()


def solution(mesh):
    n = mesh.shape["region"]

    def per_device(tokens, ln_gain, w_qkv, w_out, neighbours, degree):
        rows, width = tokens.shape
        npat = neighbours.shape[0]
        patch = rows // npat
        feat = w_qkv.shape[2]
        levels = tree_levels(n)
        ngroup = npat // GROUP
        slots = npat + 4 * RIM + 1
        hbm = pl.BlockSpec(memory_space=pltpu.HBM)
        smem = pl.BlockSpec(memory_space=pltpu.SMEM)
        dma = pltpu.SemaphoreType.DMA
        bf = jnp.bfloat16
        return pl.pallas_call(
            functools.partial(kernel, n),
            out_shape=pltpu.VMEM((rows, width), bf),
            in_specs=[
                hbm,
                pl.BlockSpec(memory_space=pltpu.VMEM),
                hbm,
                hbm,
                smem,
                smem,
            ],
            out_specs=pl.BlockSpec(memory_space=pl.ANY),
            scratch_shapes=[
                pltpu.VMEM((rows, width), bf),
                pltpu.VMEM((3, width, feat), bf),
                pltpu.VMEM((2, feat, width), bf),
                pltpu.VMEM((4 * RIM, patch, width), bf),
                pltpu.VMEM((2, patch // 2, width), bf),
                pltpu.VMEM((rows, feat), bf),
                pltpu.VMEM((slots, patch, feat), bf),
                pltpu.VMEM((slots, patch, feat), bf),
                pltpu.VMEM((2, rows, feat), bf),
                pltpu.VMEM((rows, width), bf),
                dma((5,)),
                dma,
                dma(((FAN - 1) * levels,)),
                dma,
                dma((2,)),
                dma((2,)),
                dma((4,)),
                dma((4,)),
                dma((4,)),
                dma((4,)),
                dma((ngroup,)),
                dma((ngroup,)),
                dma((ngroup + 1,)),
            ],
            compiler_params=pltpu.CompilerParams(
                collective_id=0, has_side_effects=True, vmem_limit_bytes=60 * 2**20
            ),
            name="patch_attention",
        )(
            tokens,
            ln_gain,
            jnp.transpose(w_qkv, (1, 0, 2)),
            w_out,
            jnp.transpose(neighbours),
            degree,
        )

    placed = (
        P("region", None),
        P(),
        P(None, None, "mp"),
        P("mp", None),
        P("region", None),
        P("region"),
    )
    return jax.shard_map(
        per_device, mesh=mesh, in_specs=placed, out_specs=P("region", None), check_vma=False
    )
```

```python
import functools

import jax
import jax.numpy as jnp
from jax import lax
from jax.experimental import pallas as pl
from jax.experimental.pallas import tpu as pltpu
from jax.sharding import PartitionSpec as P

HDIM = 64
NBR = 8
RIM = 2
GROUP = 4
FAN = 4
EARLY = 2
MESH = pl.DeviceIdType.MESH


def tree_levels(n):
    levels = 1
    while FAN**levels < n:
        levels += 1
    return levels


def kernel(
    n,
    tok_hbm,
    gain_ref,
    wqkv_hbm,
    wout_hbm,
    nbr_ref,
    deg_ref,
    out_hbm,
    tok,
    wqkv,
    wout,
    far_raw,
    anc_raw,
    q_tab,
    k_tab,
    v_tab,
    ctx,
    out,
    load_sem,
    anc_sem,
    anc_send,
    anc_recv,
    pair_send,
    pair_recv,
    far_send,
    far_recv,
    fwd_send,
    fwd_recv,
    ctx_send,
    ctx_recv,
    out_sem,
):
    rows, width = tok.shape
    patch = far_raw.shape[1]
    npat = rows // patch
    feat = q_tab.shape[1]
    half = patch // 2
    levels = tree_levels(n)
    far_n = 4 * RIM
    anchor_slot = npat + far_n
    region = lax.axis_index("region")
    core = lax.axis_index("mp")
    other = 1 - core

    chunk = 8 * patch
    nchunk = rows // chunk
    loads = [pltpu.make_async_copy(tok_hbm, tok, load_sem.at[0])]
    for j in range(3):
        loads.append(pltpu.make_async_copy(wqkv_hbm.at[j], wqkv.at[j], load_sem.at[1 + j]))
    loads.append(pltpu.make_async_copy(wout_hbm, wout.at[core], load_sem.at[4]))
    for c in loads:
        c.start()

    ring = [lax.rem(region + d + n, n) for d in (1, 2, -1, -2)]
    children, parents = [], []
    depth = jnp.int32(0)
    for level in range(levels):
        step = FAN**level
        digit = lax.rem(region // step, FAN)
        depth = depth + (digit > 0).astype(jnp.int32)
        alone = lax.rem(region, step) == 0
        for j in range(1, FAN):
            target = region + j * step
            children.append((jnp.logical_and(lax.rem(region, step * FAN) == 0, target < n), target))
            parents.append((jnp.logical_and(alone, digit == j), region - j * step))
    near = region < EARLY

    barrier = pltpu.get_barrier_semaphore()
    for target in ring:
        pl.semaphore_signal(barrier, inc=1, device_id=(target, core), device_id_type=MESH)
    pl.semaphore_signal(barrier, inc=1, device_id=(region, other), device_id_type=MESH)
    links = jnp.int32(5)
    for there, target in children + parents:
        links = links + there.astype(jnp.int32)

        @pl.when(there)
        def _():
            pl.semaphore_signal(barrier, inc=1, device_id=(target, core), device_id_type=MESH)

    def anc_copy(j):
        return pltpu.make_async_remote_copy(
            src_ref=anc_raw.at[core],
            dst_ref=anc_raw.at[core],
            send_sem=anc_send.at[j],
            recv_sem=anc_recv,
            device_id=(lax.rem(children[j][1], n), core),
            device_id_type=MESH,
        )

    def pair_copy(which):
        return pltpu.make_async_remote_copy(
            src_ref=anc_raw.at[which],
            dst_ref=anc_raw.at[which],
            send_sem=pair_send.at[0],
            recv_sem=pair_recv.at[0],
            device_id=(region, other),
            device_id_type=MESH,
        )

    def wout_copy(which):
        return pltpu.make_async_remote_copy(
            src_ref=wout_hbm,
            dst_ref=wout.at[which],
            send_sem=pair_send.at[1],
            recv_sem=pair_recv.at[1],
            device_id=(region, other),
            device_id_type=MESH,
        )

    def far_copy(d):
        first = (npat - RIM if d < 2 else 0) + core
        return pltpu.make_async_remote_copy(
            src_ref=tok_hbm.at[pl.ds(pl.multiple_of(first * patch, patch), patch)],
            dst_ref=far_raw.at[d * RIM + core],
            send_sem=far_send.at[d],
            recv_sem=far_recv.at[d],
            device_id=(ring[d], core),
            device_id_type=MESH,
        )

    def fwd_copy(d, which):
        return pltpu.make_async_remote_copy(
            src_ref=far_raw.at[d * RIM + which],
            dst_ref=far_raw.at[d * RIM + which],
            send_sem=fwd_send.at[d],
            recv_sem=fwd_recv.at[d],
            device_id=(region, other),
            device_id_type=MESH,
        )

    size = GROUP * patch

    def ctx_copy(g, which):
        span = pl.ds(pl.multiple_of(g * size, size), size)
        return pltpu.make_async_remote_copy(
            src_ref=ctx.at[which, span],
            dst_ref=ctx.at[which, span],
            send_sem=ctx_send.at[g],
            recv_sem=ctx_recv.at[g],
            device_id=(region, other),
            device_id_type=MESH,
        )

    def send_anchor():
        for j in reversed(range(len(children))):

            @pl.when(children[j][0])
            def _():
                anc_copy(j).start()

        pair_copy(core).start()

    def send_far():
        for d in range(4):
            far_copy(d).start()

    def enter():
        pl.semaphore_wait(barrier, links)

        @pl.when(region == 0)
        def _():
            mine = pltpu.make_async_copy(
                tok_hbm.at[pl.ds(pl.multiple_of(core * half, half), half)], anc_raw.at[core], anc_sem
            )
            mine.start()
            mine.wait()
            send_anchor()

        send_far()
        wout_copy(core).start()

    def relay():
        anc_copy(0).wait_recv()
        send_anchor()

    gain = gain_ref[...].astype(jnp.float32)

    def normalise(raw):
        values = raw.astype(jnp.float32)
        centre = jnp.mean(values, axis=-1, keepdims=True)
        away = values - centre
        spread = jnp.mean(away * away, axis=-1, keepdims=True)
        return (away * lax.rsqrt(spread + 1e-05) * gain).astype(jnp.bfloat16)

    def key_value(normed, first, count):
        for tab, j in ((k_tab, 1), (v_tab, 2)):
            part = jnp.dot(normed, wqkv[j], preferred_element_type=jnp.float32)
            tab[pl.ds(first, count)] = part.astype(jnp.bfloat16).reshape(count, patch, feat)

    enter_at = jnp.where(near, nchunk - 1, 0)
    relay_at = jnp.where(near, nchunk - 1, jnp.minimum(depth - 1, nchunk - 1))

    def qkv_step(i, carry):
        @pl.when(i == enter_at)
        def _():
            enter()

        @pl.when(i == 0)
        def _():
            for c in loads:
                c.wait()

        span = pl.ds(pl.multiple_of(i * chunk, chunk), chunk)
        normed = normalise(tok[span])
        part = jnp.dot(normed, wqkv[0], preferred_element_type=jnp.float32)
        q_tab[span] = (part * (1.0 / HDIM**0.5)).astype(jnp.bfloat16)
        key_value(normed, i * 8, 8)

        @pl.when(jnp.logical_and(i == relay_at, region > 0))
        def _():
            relay()

        return carry

    lax.fori_loop(0, nchunk, qkv_step, 0)

    pair_copy(other).wait_recv()
    key_value(normalise(anc_raw[...].reshape(patch, width)), anchor_slot, 1)

    block = GROUP * HDIM
    keys = (NBR + 2) * patch
    lane = lax.broadcasted_iota(jnp.int32, (patch, block), 1) // HDIM
    column = lax.broadcasted_iota(jnp.int32, (1, keys), 1)

    def attend(t):
        p = lax.rem(t + RIM, npat)
        deg = deg_ref[p]
        slots = [p]
        for j in range(NBR):
            nb = nbr_ref[j, p]
            owner, local = nb // npat, lax.rem(nb, npat)
            reach = lax.rem(owner - region + n, n)
            slot = jnp.where(
                reach == 0,
                local,
                jnp.where(
                    reach == n - 1,
                    local + RIM,
                    jnp.where(
                        reach == n - 2,
                        local + 2 * RIM,
                        jnp.where(reach == 1, npat + 2 * RIM + local, npat + 3 * RIM + local),
                    ),
                ),
            )
            slots.append(jnp.where(j < deg, slot, p))
        slots.append(anchor_slot)
        valid = jnp.logical_or(column < (deg + 1) * patch, column >= (NBR + 1) * patch)
        at = pl.ds(pl.multiple_of(p * patch, patch), patch)
        to = pl.ds(pl.multiple_of(t * patch, patch), patch)
        for b in range(feat // block):
            cols = slice(b * block, (b + 1) * block)
            qb = q_tab[at, cols]
            zero = jnp.zeros_like(qb)
            spread = jnp.concatenate([jnp.where(lane == i, qb, zero) for i in range(GROUP)], axis=0)
            kk = jnp.concatenate([k_tab[s, :, cols] for s in slots], axis=0)
            vv = jnp.concatenate([v_tab[s, :, cols] for s in slots], axis=0)
            scores = lax.dot_general(
                spread, kk, (((1,), (1,)), ((), ())), preferred_element_type=jnp.float32
            )
            scores = jnp.where(valid, scores, jnp.float32(-1e30))
            top = jnp.max(scores, axis=-1, keepdims=True)
            expo = jnp.exp(scores - top)
            total = jnp.sum(expo, axis=-1, keepdims=True)
            mixed = jnp.dot(expo.astype(jnp.bfloat16), vv, preferred_element_type=jnp.float32) / total
            packed = jnp.where(lane == 0, mixed[:patch], 0.0)
            for i in range(1, GROUP):
                packed = jnp.where(lane == i, mixed[i * patch : (i + 1) * patch], packed)
            ctx[core, to, cols] = packed.astype(jnp.bfloat16)

    rim_rows = RIM * patch

    def project(g):
        span = pl.ds(pl.multiple_of(g * size, size), size)
        ctx_copy(g, other).wait_recv()
        total = jnp.dot(ctx[0, span], wout[0], preferred_element_type=jnp.float32)
        total = total + jnp.dot(ctx[1, span], wout[1], preferred_element_type=jnp.float32)
        out[span] = total.astype(jnp.bfloat16)

    def inner_out(g):
        return pltpu.make_async_copy(
            out.at[pl.ds(pl.multiple_of(g * size, size), size)],
            out_hbm.at[pl.ds(pl.multiple_of(g * size + rim_rows, rim_rows), size)],
            out_sem.at[g],
        )

    ngroup = npat // GROUP

    def swap_far():
        for d in range(4):
            far_copy(d).wait_recv()
            fwd_copy(d, core).start()
        wout_copy(other).wait_recv()

    def far_step(d, c):
        raw = far_raw[pl.ds(d * 2 * RIM, 2 * RIM)].reshape(2 * rim_rows, width)
        key_value(normalise(raw), npat + d * 2 * RIM, 2 * RIM)
        return c

    def group_step(g, carry):
        @pl.when(g == 1)
        def _():
            swap_far()

        @pl.when(g == ngroup - 1)
        def _():
            for d in range(4):
                fwd_copy(d, other).wait_recv()
            lax.fori_loop(0, 2, far_step, 0)

        def patch_step(u, c):
            attend(g * GROUP + u)
            return c

        lax.fori_loop(0, GROUP, patch_step, 0, unroll=4)
        ctx_copy(g, core).start()

        @pl.when(g >= 1)
        def _():
            project(g - 1)
            inner_out(g - 1).start()

        return carry

    lax.fori_loop(0, ngroup, group_step, 0)
    project(ngroup - 1)
    tail = rows - size
    last = [
        pltpu.make_async_copy(
            out.at[pl.ds(tail, rim_rows)], out_hbm.at[pl.ds(rows - rim_rows, rim_rows)], out_sem.at[ngroup - 1]
        ),
        pltpu.make_async_copy(
            out.at[pl.ds(tail + rim_rows, rim_rows)], out_hbm.at[pl.ds(0, rim_rows)], out_sem.at[ngroup]
        ),
    ]
    for c in last:
        c.start()

    for j in range(len(children)):

        @pl.when(children[j][0])
        def _():
            anc_copy(j).wait_send()

    pair_copy(core).wait_send()
    wout_copy(core).wait_send()
    for d in range(4):
        far_copy(d).wait_send()
        fwd_copy(d, core).wait_send()
    for g in range(ngroup):
        ctx_copy(g, core).wait_send()
    for g in range(ngroup - 1):
        inner_out(g).wait()
    for c in last:
        c.wait()


def solution(mesh):
    n = mesh.shape["region"]

    def per_device(tokens, ln_gain, w_qkv, w_out, neighbours, degree):
        rows, width = tokens.shape
        npat = neighbours.shape[0]
        patch = rows // npat
        feat = w_qkv.shape[2]
        levels = tree_levels(n)
        ngroup = npat // GROUP
        slots = npat + 4 * RIM + 1
        hbm = pl.BlockSpec(memory_space=pltpu.HBM)
        smem = pl.BlockSpec(memory_space=pltpu.SMEM)
        dma = pltpu.SemaphoreType.DMA
        bf = jnp.bfloat16
        return pl.pallas_call(
            functools.partial(kernel, n),
            out_shape=pltpu.VMEM((rows, width), bf),
            in_specs=[
                hbm,
                pl.BlockSpec(memory_space=pltpu.VMEM),
                hbm,
                hbm,
                smem,
                smem,
            ],
            out_specs=pl.BlockSpec(memory_space=pl.ANY),
            scratch_shapes=[
                pltpu.VMEM((rows, width), bf),
                pltpu.VMEM((3, width, feat), bf),
                pltpu.VMEM((2, feat, width), bf),
                pltpu.VMEM((4 * RIM, patch, width), bf),
                pltpu.VMEM((2, patch // 2, width), bf),
                pltpu.VMEM((rows, feat), bf),
                pltpu.VMEM((slots, patch, feat), bf),
                pltpu.VMEM((slots, patch, feat), bf),
                pltpu.VMEM((2, rows, feat), bf),
                pltpu.VMEM((rows, width), bf),
                dma((5,)),
                dma,
                dma(((FAN - 1) * levels,)),
                dma,
                dma((2,)),
                dma((2,)),
                dma((4,)),
                dma((4,)),
                dma((4,)),
                dma((4,)),
                dma((ngroup,)),
                dma((ngroup,)),
                dma((ngroup + 1,)),
            ],
            compiler_params=pltpu.CompilerParams(
                collective_id=0, has_side_effects=True, vmem_limit_bytes=60 * 2**20
            ),
            name="patch_attention",
        )(
            tokens,
            ln_gain,
            jnp.transpose(w_qkv, (1, 0, 2)),
            w_out,
            jnp.transpose(neighbours),
            degree,
        )

    placed = (
        P("region", None),
        P(),
        P(None, None, "mp"),
        P("mp", None),
        P("region", None),
        P("region"),
    )
    return jax.shard_map(
        per_device, mesh=mesh, in_specs=placed, out_specs=P("region", None), check_vma=False
    )
```
